32 devices in a mesh: ma: 16 (over z, y, core), freq: 2 (over x).
Axes of the slice: x: 2, y: 2, z: 4, core: 2. Of those that a mesh axis runs over, the one named last changes fastest.
Arguments:
- right_side: float32 [128, 8, 2, 512], P('ma', 'freq'), may hold values from -60 to 60
- start_field: float32 [128, 8, 2, 512], P('ma', 'freq'), may hold values from -6 to 6
- beam: float32 [128, 8, 2, 16, 512], P('ma', 'freq'), may hold values from -0.75 to 0.75
- noise: float32 [128, 8, 16], P('ma', 'freq'), may hold values from 0.3 to 3
- inv_power: float32 [512], replicated, may hold values from 0.5 to 2
- smooth: float32 [512], replicated, may hold values from 0.5 to 4
Outputs:
- solution_field: float32 [128, 8, 2, 512], P('ma', 'freq')
- residual: float32 [128, 8, 2, 512], P('ma', 'freq')
The draws below stay inside these ranges and needn't reach their ends.
All inputs are finite; a program needn't handle non-finite values.
Results may differ from the reference program's by a relative error of at most 0.0003.
Values sent between devices are 32-bit elements; how exact they have to be, the bound alone decides.
A program may use at most 64 MiB of HBM per device.

```python
import math
import jax
import jax.numpy as jnp
from jax import lax

ELL = 512
RANK = 16
ITERS = 2
M = 128
FREQ = 8


def draw_right_side(key, part):
    key_values = jax.random.fold_in(key, 0)
    position = jnp.arange(M, dtype=jnp.float32) / M
    row_scale = jnp.power(10.0, position)
    values = jnp.clip(jax.random.normal(key_values, (M, FREQ, 2, ELL), jnp.float32), -6.0, 6.0)
    return jnp.clip(values * row_scale[:, None, None, None], -60.0, 60.0)


def block_scale(own_key, dims, pieces, low, largest):
    loudness, own = 1.0, jax.random.fold_in(own_key, 6)
    for axis_at, shards_of in pieces:
        draws = jnp.exp(jax.random.uniform(jax.random.fold_in(own, axis_at), (shards_of,), jnp.float32, low / len(pieces), largest / len(pieces)))
        loudness = loudness * jnp.repeat(draws, dims[axis_at] // shards_of).reshape([-1 if axis == axis_at else 1 for axis in range(len(dims))])
    return loudness


def gaussian(own_key, dims, spread, reach, cuts=(), held_as=jnp.bfloat16):
    drawn = spread * jax.random.normal(own_key, dims, jnp.float32)
    if cuts:
        drawn = drawn * block_scale(own_key, dims, cuts, -0.22, 0.18)
    return jnp.clip(drawn, -reach, reach).astype(held_as)


def setup_inputs(seed: int = 0) -> dict:
    splits = jax.random.split(jax.random.key(seed), 7)
    return {
        "right_side": draw_right_side(jax.random.fold_in(splits[6], 71), 0),
        "start_field": gaussian(splits[1], (M, FREQ, 2, ELL), 1.0, 6.0, ((0, 16), (1, 2)), jnp.float32),
        "beam": gaussian(splits[2], (M, FREQ, 2, RANK, ELL), (4 * RANK) ** -0.5, 0.75, ((0, 16), (1, 2)), jnp.float32),
        "noise": jnp.clip(jnp.exp(math.log(3.0) - 2.3025851 * jax.random.uniform(splits[3], (M, FREQ, RANK), jnp.float32) ** block_scale(splits[3], (M, FREQ, RANK), ((0, 16), (1, 2)), -0.2, 0.2)), 0.3, 3.0),
        "inv_power": jnp.clip(jnp.exp(jax.random.uniform(splits[4], (ELL,), jnp.float32, math.log(0.5), math.log(2.0))), 0.5, 2.0),
        "smooth": jnp.clip(jnp.exp(jax.random.uniform(splits[5], (ELL,), jnp.float32, math.log(0.5), math.log(4.0))), 0.5, 4.0),
    }


def beam_image(field, beam, noise):
    projected = jnp.einsum('mfakl,mfbl->mfabk', beam, field, precision=lax.Precision.HIGHEST)
    real_part = projected[:, :, 0, 0] + projected[:, :, 1, 1]
    imaginary = projected[:, :, 0, 1] - projected[:, :, 1, 0]
    weighted = jnp.stack([real_part, imaginary], axis=2) * noise[:, :, None, :]
    back = jnp.einsum('mfakl,mfbk->mfabl', beam, weighted, precision=lax.Precision.HIGHEST)
    return jnp.stack([back[:, :, 0, 0] - back[:, :, 1, 1], back[:, :, 0, 1] + back[:, :, 1, 0]], axis=2)


def operate(field, beam, noise, inv_power, smooth):
    padded = jnp.pad(field, ((0, 0), (1, 1), (0, 0), (0, 0)))
    channel = jnp.arange(field.shape[1], dtype=jnp.int32)
    weight = (channel > 0).astype(jnp.float32) + (channel < field.shape[1] - 1).astype(jnp.float32)
    prior = smooth * (weight[None, :, None, None] * field - padded[:, :-2] - padded[:, 2:])
    return beam_image(field, beam, noise) + inv_power * field + prior


def reference(right_side, start_field, beam, noise, inv_power, smooth):
    solution_field = start_field
    resid_now = right_side - operate(start_field, beam, noise, inv_power, smooth)
    direction = resid_now
    norm_now = jnp.sum(resid_now * resid_now)
    for turn in range(ITERS):
        applied = operate(direction, beam, noise, inv_power, smooth)
        step_size = norm_now / jnp.sum(direction * applied)
        solution_field = solution_field + step_size * direction
        resid_now = resid_now - step_size * applied
        norm_next = jnp.sum(resid_now * resid_now)
        direction = resid_now + (norm_next / norm_now) * direction
        norm_now = norm_next
    return solution_field, resid_now
```

```python
import functools

import jax
import jax.numpy as jnp
from jax import lax
from jax.experimental import pallas as pl
from jax.experimental.pallas import tpu as pltpu
from jax.sharding import PartitionSpec as P

MESH = pl.DeviceIdType.MESH
F32, BF16 = jnp.float32, jnp.bfloat16


def split(x):
    high = x.astype(BF16)
    return high, (x - high.astype(F32)).astype(BF16)


def times(x, high, low, transposed):
    dims = (((1,), (1 if transposed else 0,)), ((), ()))
    rows = x.shape[0]
    x_high, x_low = split(x)
    both = jnp.concatenate([x_high, x_low], axis=0)
    main = lax.dot_general(both, high, dims, preferred_element_type=F32)
    rest = lax.dot_general(x_high, low, dims, preferred_element_type=F32)
    return main[:rows] + (main[rows:] + rest)


def kernel(
    nma, nf, rhs_in, x0_in, beam_in, noise_in, power_in, smooth_in, sol_out, res_out,
    rhs_s, x0_s, beam_s, noise_s, power_s, smooth_s, sol_s, res_s,
    high_s, low_s, x_s, y_s, r_s, u_s, w_s, mask_s, halo_s, message_s, all_s,
    in_sem, beam_sem, out_sem, halo_send, halo_recv, sum_send, sum_recv,
):
    modes, freqs, _, ell = rhs_in.shape
    rank = beam_in.shape[3]
    width = modes * rank
    n = nma * nf
    my_ma, my_f = lax.axis_index("ma"), lax.axis_index("freq")
    me = my_ma * nf + my_f
    last = freqs - 1
    order = [last] + ([0] if last else []) + list(range(1, last))

    x0_copy = pltpu.make_async_copy(x0_in, x0_s, in_sem.at[0])
    small = [
        pltpu.make_async_copy(power_in, power_s, in_sem.at[1]),
        pltpu.make_async_copy(smooth_in, smooth_s, in_sem.at[2]),
        pltpu.make_async_copy(noise_in, noise_s, in_sem.at[3]),
    ]
    rhs_copy = pltpu.make_async_copy(rhs_in, rhs_s, in_sem.at[4])
    x0_copy.start()
    for copy in small:
        copy.start()
    beam_copies = {}
    for i, f in enumerate(order):
        beam_copies[f] = [
            pltpu.make_async_copy(beam_in.at[:, f, a], beam_s.at[f, a], beam_sem.at[2 * f + a])
            for a in range(2)
        ]
        for copy in beam_copies[f]:
            copy.start()
        if i == 0:
            rhs_copy.start()

    def target(offset):
        ma = my_ma + offset // nf
        other = my_f + offset % nf
        return lax.rem(ma, nma), lax.rem(other, nf)

    barrier = pltpu.get_barrier_semaphore()

    def greet(offset, carry):
        pl.semaphore_signal(barrier, inc=1, device_id=target(offset), device_id_type=MESH)
        return carry

    if n > 64:
        lax.fori_loop(1, n, greet, 0)
    else:
        for offset in range(1, n):
            greet(offset, 0)

    has_left, has_right = my_f > 0, my_f < nf - 1

    def halo_copies(kind, source):
        to_right = pltpu.make_async_remote_copy(
            src_ref=source.at[last], dst_ref=halo_s.at[kind, 0],
            send_sem=halo_send.at[kind, 1], recv_sem=halo_recv.at[kind, 0],
            device_id=(my_ma, my_f + 1), device_id_type=MESH,
        )
        to_left = pltpu.make_async_remote_copy(
            src_ref=source.at[0], dst_ref=halo_s.at[kind, 1],
            send_sem=halo_send.at[kind, 0], recv_sem=halo_recv.at[kind, 1],
            device_id=(my_ma, my_f - 1), device_id_type=MESH,
        )
        return to_right, to_left

    def send(kind, source):
        to_right, to_left = halo_copies(kind, source)
        if nf > 1:
            pl.when(has_right)(to_right.start)
            pl.when(has_left)(to_left.start)

    def arrive(kind, source):
        to_right, to_left = halo_copies(kind, source)
        if nf > 1:
            pl.when(has_left)(to_right.wait_recv)
            pl.when(has_right)(to_left.wait_recv)

    def sent(kind, source):
        to_right, to_left = halo_copies(kind, source)
        if nf > 1:
            pl.when(has_right)(to_right.wait_send)
            pl.when(has_left)(to_left.wait_send)

    @pl.when(jnp.logical_not(has_left))
    def _():
        halo_s[:, 0] = jnp.zeros_like(halo_s[:, 0])

    @pl.when(jnp.logical_not(has_right))
    def _():
        halo_s[:, 1] = jnp.zeros_like(halo_s[:, 1])

    x0_copy.wait()
    for f in range(freqs):
        for b in range(2):
            x_s[f, b * modes:(b + 1) * modes, :] = x0_s[:, f, b, :]
    for copy in small:
        copy.wait()
    pl.semaphore_wait(barrier, n - 1)
    send(0, x_s)

    power, smooth = power_s[...], smooth_s[...]
    own = (
        lax.broadcasted_iota(jnp.int32, (modes, width), 1) // rank
        == lax.broadcasted_iota(jnp.int32, (modes, width), 0)
    )
    for f in range(freqs):
        mask_s[f] = jnp.where(own, jnp.concatenate([noise_s[:, f, :]] * modes, axis=1), 0.0)

    def project(f, field):
        seen = times(field, high_s[f], low_s[f], True)
        real = seen[:modes, :width] + seen[modes:, width:]
        imaginary = seen[modes:, :width] - seen[:modes, width:]
        return real, imaginary, mask_s[f] * real, mask_s[f] * imaginary

    def back(f, real, imaginary):
        weighted = jnp.concatenate(
            [
                jnp.concatenate([real, -imaginary], axis=1),
                jnp.concatenate([imaginary, real], axis=1),
            ],
            axis=0,
        )
        return times(weighted, high_s[f], low_s[f], False)

    def count(f):
        below = jnp.where(has_left, 1.0, 0.0) if f == 0 else 1.0
        above = jnp.where(has_right, 1.0, 0.0) if f == last else 1.0
        return below + above

    def local_prior(f, ref):
        value = count(f) * ref[f]
        if f > 0:
            value = value - ref[f - 1]
        if f < last:
            value = value - ref[f + 1]
        return power * ref[f] + smooth * value

    def apply_beam(f, field):
        _, _, real, imaginary = project(f, field)
        return back(f, real, imaginary)

    for f in order:
        for copy in beam_copies[f]:
            copy.wait()
        high, low = split(beam_s[f].reshape(2 * width, ell))
        high_s[f] = high
        low_s[f] = low
        if f == order[0]:
            rhs_copy.wait()
        rhs = jnp.concatenate([rhs_s[:, f, 0, :], rhs_s[:, f, 1, :]], axis=0)
        y_s[f] = rhs - apply_beam(f, x_s[f]) - local_prior(f, x_s)
        if f == 0:
            send(1, y_s)
    inner = list(range(1, last))
    outer = [f for f in order if f not in inner]
    for f in inner:
        r_s[f] = y_s[f]
    for f in inner:
        u_s[f] = apply_beam(f, r_s[f])
    arrive(0, x_s)
    arrive(1, y_s)
    for f in outer:
        value = y_s[f]
        if f == 0:
            value = value + smooth * halo_s[0, 0]
        if f == last:
            value = value + smooth * halo_s[0, 1]
        r_s[f] = value
    before = jnp.where(has_left, halo_s[1, 0] + smooth * x_s[0], 0.0)
    after = jnp.where(has_right, halo_s[1, 1] + smooth * x_s[last], 0.0)
    for f in outer:
        value = apply_beam(f, r_s[f]) + local_prior(f, r_s)
        if f == 0:
            value = value - smooth * before
        if f == last:
            value = value - smooth * after
        u_s[f] = value
    send(2, u_s)
    for f in inner:
        u_s[f] = u_s[f] + local_prior(f, r_s)
    norm = jnp.zeros((2 * modes, ell), F32)
    curve, square, cube = norm, norm, norm
    beam_part = jnp.zeros((modes, width), F32)
    pending = {}
    for f in inner + outer:
        real, imaginary, real_weighted, imaginary_weighted = project(f, u_s[f])
        pending[f] = real_weighted, imaginary_weighted
        beam_part = beam_part + (real * real_weighted + imaginary * imaginary_weighted)
        w_s[f] = local_prior(f, u_s)
        norm = norm + r_s[f] * r_s[f]
        curve = curve + r_s[f] * u_s[f]
        square = square + u_s[f] * u_s[f]
        cube = cube + u_s[f] * w_s[f]
    arrive(2, u_s)
    before, after = smooth * halo_s[2, 0], smooth * halo_s[2, 1]
    cube = cube - (before * u_s[0] + after * u_s[last])
    lane = lax.broadcasted_iota(jnp.int32, (1, 128), 1)
    message = jnp.zeros((1, 128), F32)
    for i, part in enumerate((norm, curve, square, cube)):
        total = jnp.sum(part, keepdims=True)
        if i == 3:
            total = total + jnp.sum(beam_part, keepdims=True)
        message = jnp.where(lane == i, total, message)
    message_s[0] = message
    all_s[me] = message

    def share(offset, carry):
        pltpu.make_async_remote_copy(
            src_ref=message_s.at[0], dst_ref=all_s.at[me], send_sem=sum_send, recv_sem=sum_recv,
            device_id=target(offset), device_id_type=MESH,
        ).start()
        return carry

    if n > 64:
        lax.fori_loop(1, n, share, 0)
    else:
        for offset in range(1, n):
            share(offset, 0)

    w_s[0] = w_s[0] - before
    w_s[last] = w_s[last] - after
    for f in range(freqs):
        w_s[f] = w_s[f] + back(f, *pending[f])
    for kind, source in enumerate((x_s, y_s, u_s)):
        sent(kind, source)
    if n > 1:
        everything = all_s.at[pl.ds(0, n - 1)]
        pltpu.make_async_copy(everything, everything, sum_recv).wait()
    total = jnp.sum(all_s[...], axis=0)
    m0, m1, m2, m3 = (total[:, i:i + 1] for i in range(4))
    step = m0 / m1
    norm_next = step * (step * m2 - m1)
    curve_next = m1 - 2.0 * step * m2 + step * step * m3
    growth = norm_next / m0
    step_next = norm_next / (curve_next - growth * norm_next / step)
    c = step + step_next * (1.0 + growth)
    e = step * step_next
    for f in range(freqs):
        solved = x_s[f] + c * r_s[f] - e * u_s[f]
        left = r_s[f] - c * u_s[f] + e * w_s[f]
        for b in range(2):
            sol_s[:, f, b, :] = solved[b * modes:(b + 1) * modes]
            res_s[:, f, b, :] = left[b * modes:(b + 1) * modes]
    outs = [
        pltpu.make_async_copy(sol_s, sol_out, out_sem.at[0]),
        pltpu.make_async_copy(res_s, res_out, out_sem.at[1]),
    ]
    for copy in outs:
        copy.start()
    if n > 1:
        everything = all_s.at[pl.ds(0, n - 1)]
        pltpu.make_async_copy(everything, everything, sum_send).wait()
    for copy in outs:
        copy.wait()


def shards(right_side, start_field, beam, noise, inv_power, smooth):
    nma, nf = lax.axis_size("ma"), lax.axis_size("freq")
    modes, freqs, _, ell = right_side.shape
    rank = beam.shape[3]
    width = modes * rank
    any_spec = pl.BlockSpec(memory_space=pl.ANY)
    field = pltpu.VMEM(right_side.shape, F32)
    slab = pltpu.VMEM((freqs, 2 * modes, ell), F32)
    half = pltpu.VMEM((freqs, 2 * width, ell), BF16)
    return pl.pallas_call(
        functools.partial(kernel, nma, nf),
        out_shape=[jax.ShapeDtypeStruct(right_side.shape, F32)] * 2,
        in_specs=[any_spec] * 6,
        out_specs=[any_spec] * 2,
        scratch_shapes=[
            field, field,
            pltpu.VMEM((freqs, 2, modes, rank, ell), F32),
            pltpu.VMEM(noise.shape, F32),
            pltpu.VMEM((1, ell), F32), pltpu.VMEM((1, ell), F32),
            field, field,
            half, half,
            slab, slab, slab, slab, slab,
            pltpu.VMEM((freqs, modes, width), F32),
            pltpu.VMEM((3, 2, 2 * modes, ell), F32),
            pltpu.VMEM((1, 1, 128), F32),
            pltpu.VMEM((nma * nf, 1, 128), F32),
            pltpu.SemaphoreType.DMA((5,)),
            pltpu.SemaphoreType.DMA((2 * freqs,)),
            pltpu.SemaphoreType.DMA((2,)),
            pltpu.SemaphoreType.DMA((3, 2)),
            pltpu.SemaphoreType.DMA((3, 2)),
            pltpu.SemaphoreType.DMA,
            pltpu.SemaphoreType.DMA,
        ],
        compiler_params=pltpu.CompilerParams(collective_id=0, has_side_effects=True),
        name="solve",
    )(right_side, start_field, beam, noise, inv_power[None], smooth[None])


def solution(mesh):
    in_specs = (
        P("ma", "freq", None, None),
        P("ma", "freq", None, None),
        P("ma", "freq", None, None, None),
        P("ma", "freq", None),
        P(),
        P(),
    )
    out_specs = (P("ma", "freq", None, None), P("ma", "freq", None, None))
    return jax.shard_map(shards, mesh=mesh, in_specs=in_specs, out_specs=out_specs, check_vma=False)
```

```python
import functools

import jax
import jax.numpy as jnp
from jax import lax
from jax.experimental import pallas as pl
from jax.experimental.pallas import tpu as pltpu
from jax.sharding import PartitionSpec as P

MESH = pl.DeviceIdType.MESH
F32, BF16 = jnp.float32, jnp.bfloat16


def split(x):
    high = x.astype(BF16)
    return high, (x - high.astype(F32)).astype(BF16)


def times(x, high, low, transposed):
    dims = (((1,), (1 if transposed else 0,)), ((), ()))
    rows = x.shape[0]
    x_high, x_low = split(x)
    both = jnp.concatenate([x_high, x_low], axis=0)
    main = lax.dot_general(both, high, dims, preferred_element_type=F32)
    rest = lax.dot_general(x_high, low, dims, preferred_element_type=F32)
    return main[:rows] + (main[rows:] + rest)


def kernel(
    nma, nf, rhs_in, x0_in, beam_in, noise_in, power_in, smooth_in, sol_s, res_s,
    rhs_s, x0_s, beam_s, noise_s, power_s, smooth_s,
    high_s, low_s, x_s, y_s, r_s, u_s, w_s, mask_s, halo_s, message_s, all_s,
    in_sem, beam_sem, halo_send, halo_recv, sum_send, sum_recv, word_sem,
):
    modes, freqs, _, ell = rhs_in.shape
    rank = beam_in.shape[3]
    width = modes * rank
    n = nma * nf
    my_ma, my_f = lax.axis_index("ma"), lax.axis_index("freq")
    me = my_ma * nf + my_f
    last = freqs - 1
    two_sided = nf > 2

    def at(g):
        return jnp.where(my_f == 0, last - g, g)


    x0_copy = pltpu.make_async_copy(x0_in, x0_s, in_sem.at[0])
    small = [
        pltpu.make_async_copy(power_in, power_s, in_sem.at[1]),
        pltpu.make_async_copy(smooth_in, smooth_s, in_sem.at[2]),
        pltpu.make_async_copy(noise_in, noise_s, in_sem.at[3]),
    ]
    rhs_copy = pltpu.make_async_copy(rhs_in, rhs_s, in_sem.at[4])
    x0_copy.start()
    for copy in small:
        copy.start()
    beam_copies = {}
    for f in range(freqs):
        beam_copies[f] = [
            pltpu.make_async_copy(beam_in.at[:, at(f), a], beam_s.at[f, a], beam_sem.at[2 * f + a])
            for a in range(2)
        ]
        for copy in beam_copies[f]:
            copy.start()
        if f == 0:
            rhs_copy.start()

    def target(offset):
        ma = my_ma + offset // nf
        other = my_f + offset % nf
        return lax.rem(ma, nma), lax.rem(other, nf)

    def partners(size, place):
        distances = [1 << bit for bit in range(size.bit_length() - 1)]
        return [place + d * (1 - 2 * (place // d % 2)) for d in distances]

    word = [(my_ma, other) for other in partners(nf, my_f)]
    word += [(other, my_f) for other in partners(nma, my_ma)]
    barrier = pltpu.get_barrier_semaphore()
    near = jnp.where(my_f == 0, 1, my_f - 1)
    has_far = (my_f > 0) & (my_f < nf - 1)

    def greet(device):
        pl.semaphore_signal(barrier, inc=1, device_id=device, device_id_type=MESH)

    for device in word:
        greet(device)
    expected = len(word)
    if nf > 2:
        pl.when(my_f > 0)(lambda: greet((my_ma, my_f - 1)))
        pl.when(my_f < nf - 1)(lambda: greet((my_ma, my_f + 1)))
        expected = expected + jnp.minimum(my_f, 1) + jnp.minimum(nf - 1 - my_f, 1)

    def pass_word(step):
        if step > 0:
            pl.semaphore_wait(word_sem.at[step - 1], 1)
        if step < len(word):
            pl.semaphore_signal(
                word_sem.at[step], inc=1, device_id=word[step], device_id_type=MESH
            )

    def near_copy(kind, source):
        side = jnp.minimum(my_f // 2, 1) if two_sided else 0
        return pltpu.make_async_remote_copy(
            src_ref=source.at[0], dst_ref=halo_s.at[kind, side],
            send_sem=halo_send.at[kind, 0], recv_sem=halo_recv.at[kind, side],
            device_id=(my_ma, near), device_id_type=MESH,
        )

    def far_copy(kind, source):
        return pltpu.make_async_remote_copy(
            src_ref=source.at[last], dst_ref=halo_s.at[kind, 0],
            send_sem=halo_send.at[kind, 1], recv_sem=halo_recv.at[kind, 0],
            device_id=(my_ma, my_f + 1), device_id_type=MESH,
        )

    def arrival(kind, side):
        slot = halo_s.at[kind, side]
        return pltpu.make_async_copy(slot, slot, halo_recv.at[kind, side])

    def send(kind, source):
        if nf > 1:
            near_copy(kind, source).start()
        if two_sided:
            pl.when(has_far)(lambda: far_copy(kind, source).start())

    def arrive(kind):
        if nf > 1:
            arrival(kind, 0).wait()
        if two_sided:
            pl.when(has_far)(lambda: arrival(kind, 1).wait())

    def sent(kind, source):
        if nf > 1:
            near_copy(kind, source).wait_send()
        if two_sided:
            pl.when(has_far)(lambda: far_copy(kind, source).wait_send())

    if nf == 1:
        halo_s[...] = jnp.zeros_like(halo_s)
    if two_sided:
        @pl.when(jnp.logical_not(has_far))
        def _():
            halo_s[:, 1] = jnp.zeros_like(halo_s[:, 1])

    x0_copy.wait()
    for f in range(freqs):
        for b in range(2):
            x_s[f, b * modes:(b + 1) * modes, :] = x0_s[:, at(f), b, :]
    for copy in small:
        copy.wait()
    pl.semaphore_wait(barrier, expected)
    send(0, x_s)
    pass_word(0)

    power, smooth = power_s[...], smooth_s[...]
    own = (
        lax.broadcasted_iota(jnp.int32, (modes, width), 1) // rank
        == lax.broadcasted_iota(jnp.int32, (modes, width), 0)
    )
    for f in range(freqs):
        mask_s[f] = jnp.where(own, jnp.concatenate([noise_s[:, at(f), :]] * modes, axis=1), 0.0)

    def project(f, field):
        seen = times(field, high_s[f], low_s[f], True)
        real = seen[:modes, :width] + seen[modes:, width:]
        imaginary = seen[modes:, :width] - seen[:modes, width:]
        return real, imaginary, mask_s[f] * real, mask_s[f] * imaginary

    def back(f, real, imaginary):
        weighted = jnp.concatenate(
            [
                jnp.concatenate([real, -imaginary], axis=1),
                jnp.concatenate([imaginary, real], axis=1),
            ],
            axis=0,
        )
        return times(weighted, high_s[f], low_s[f], False)

    def count(f):
        value = float(f > 0) + float(f < last) + float(nf > 1 and f == 0)
        if two_sided and f == last:
            value = value + jnp.where(has_far, 1.0, 0.0)
        return value

    def local_prior(f, ref):
        value = count(f) * ref[f]
        if f > 0:
            value = value - ref[f - 1]
        if f < last:
            value = value - ref[f + 1]
        return power * ref[f] + smooth * value

    def apply_beam(f, field):
        _, _, real, imaginary = project(f, field)
        return back(f, real, imaginary)

    edges = [0, last] if two_sided and last else [0]
    inner = [f for f in range(freqs) if f not in edges]
    for f in edges + inner:
        for copy in beam_copies[f]:
            copy.wait()
        high, low = split(beam_s[f].reshape(2 * width, ell))
        high_s[f] = high
        low_s[f] = low
        if f == 0:
            rhs_copy.wait()
        rhs = jnp.concatenate([rhs_s[:, at(f), 0, :], rhs_s[:, at(f), 1, :]], axis=0)
        y_s[f] = rhs - apply_beam(f, x_s[f]) - local_prior(f, x_s)
        if f == edges[-1]:
            send(1, y_s)
    pass_word(1)
    for f in inner:
        r_s[f] = y_s[f]
        u_s[f] = apply_beam(f, r_s[f])
    pass_word(2)
    arrive(0)
    arrive(1)
    before = after = 0.0
    r_s[0] = y_s[0] + smooth * halo_s[0, 0]
    if nf > 1:
        before = halo_s[1, 0] + smooth * x_s[0]
    if two_sided:
        base = r_s if last == 0 else y_s
        r_s[last] = base[last] + smooth * halo_s[0, 1]
        after = jnp.where(has_far, halo_s[1, 1] + smooth * x_s[last], 0.0)
    for f in edges:
        value = apply_beam(f, r_s[f]) + local_prior(f, r_s)
        if f == 0:
            value = value - smooth * before
        if f == last:
            value = value - smooth * after
        u_s[f] = value
    send(2, u_s)
    passed = 3
    for f in inner:
        u_s[f] = u_s[f] + local_prior(f, r_s)
    norm = jnp.zeros((2 * modes, ell), F32)
    curve, square, cube = norm, norm, norm
    beam_part = jnp.zeros((modes, width), F32)
    pending = {}
    for f in inner + edges:
        real, imaginary, real_weighted, imaginary_weighted = project(f, u_s[f])
        pending[f] = real_weighted, imaginary_weighted
        beam_part = beam_part + (real * real_weighted + imaginary * imaginary_weighted)
        w_s[f] = local_prior(f, u_s)
        norm = norm + r_s[f] * r_s[f]
        curve = curve + r_s[f] * u_s[f]
        square = square + u_s[f] * u_s[f]
        cube = cube + u_s[f] * w_s[f]
    arrive(2)
    before = smooth * halo_s[2, 0]
    cube = cube - before * u_s[0]
    if two_sided:
        after = smooth * halo_s[2, 1]
        cube = cube - after * u_s[last]
    lane = lax.broadcasted_iota(jnp.int32, (1, 128), 1)
    message = jnp.zeros((1, 128), F32)
    for i, part in enumerate((norm, curve, square, cube)):
        total = jnp.sum(part, keepdims=True)
        if i == 3:
            total = total + jnp.sum(beam_part, keepdims=True)
        message = jnp.where(lane == i, total, message)
    message_s[0] = message
    all_s[me] = message

    for step in range(passed, len(word) + 1):
        pass_word(step)

    def share(offset, carry):
        pltpu.make_async_remote_copy(
            src_ref=message_s.at[0], dst_ref=all_s.at[me], send_sem=sum_send, recv_sem=sum_recv,
            device_id=target(offset), device_id_type=MESH,
        ).start()
        return carry

    if n > 64:
        lax.fori_loop(1, n, share, 0)
    else:
        for offset in range(1, n):
            share(offset, 0)

    w_s[0] = w_s[0] - before
    if two_sided:
        w_s[last] = w_s[last] - after
    for f in range(freqs):
        w_s[f] = w_s[f] + back(f, *pending[f])
    for kind, source in enumerate((x_s, y_s, u_s)):
        sent(kind, source)
    if n > 1:
        everything = all_s.at[pl.ds(0, n - 1)]
        pltpu.make_async_copy(everything, everything, sum_recv).wait()
    total = jnp.sum(all_s[...], axis=0)
    m0, m1, m2, m3 = (total[:, i:i + 1] for i in range(4))
    step = m0 / m1
    norm_next = step * (step * m2 - m1)
    curve_next = m1 - 2.0 * step * m2 + step * step * m3
    growth = norm_next / m0
    step_next = norm_next / (curve_next - growth * norm_next / step)
    c = step + step_next * (1.0 + growth)
    e = step * step_next
    for f in range(freqs):
        solved = x_s[f] + c * r_s[f] - e * u_s[f]
        left = r_s[f] - c * u_s[f] + e * w_s[f]
        for b in range(2):
            sol_s[:, at(f), b, :] = solved[b * modes:(b + 1) * modes]
            res_s[:, at(f), b, :] = left[b * modes:(b + 1) * modes]
    if n > 1:
        everything = all_s.at[pl.ds(0, n - 1)]
        pltpu.make_async_copy(everything, everything, sum_send).wait()


def write_out(sol_in, res_in, sol_out, res_out, sem):
    copies = [
        pltpu.make_async_copy(sol_in, sol_out, sem.at[0]),
        pltpu.make_async_copy(res_in, res_out, sem.at[1]),
    ]
    for copy in copies:
        copy.start()
    for copy in copies:
        copy.wait()


def shards(right_side, start_field, beam, noise, inv_power, smooth):
    nma, nf = lax.axis_size("ma"), lax.axis_size("freq")
    modes, freqs, _, ell = right_side.shape
    rank = beam.shape[3]
    width = modes * rank
    vmem_spec = pl.BlockSpec(memory_space=pltpu.VMEM)
    any_spec = pl.BlockSpec(memory_space=pl.ANY)
    field = pltpu.VMEM(right_side.shape, F32)
    slab = pltpu.VMEM((freqs, 2 * modes, ell), F32)
    half = pltpu.VMEM((freqs, 2 * width, ell), BF16)
    outs = pl.pallas_call(
        functools.partial(kernel, nma, nf),
        out_shape=[field] * 2,
        in_specs=[any_spec] * 6,
        out_specs=[vmem_spec] * 2,
        scratch_shapes=[
            field, field,
            pltpu.VMEM((freqs, 2, modes, rank, ell), F32),
            pltpu.VMEM(noise.shape, F32),
            pltpu.VMEM((1, ell), F32), pltpu.VMEM((1, ell), F32),
            half, half,
            slab, slab, slab, slab, slab,
            pltpu.VMEM((freqs, modes, width), F32),
            pltpu.VMEM((3, 2, 2 * modes, ell), F32),
            pltpu.VMEM((1, 1, 128), F32),
            pltpu.VMEM((nma * nf, 1, 128), F32),
            pltpu.SemaphoreType.DMA((5,)),
            pltpu.SemaphoreType.DMA((2 * freqs,)),
            pltpu.SemaphoreType.DMA((3, 2)),
            pltpu.SemaphoreType.DMA((3, 2)),
            pltpu.SemaphoreType.DMA,
            pltpu.SemaphoreType.DMA,
            pltpu.SemaphoreType.REGULAR(((nma * nf).bit_length(),)),
        ],
        compiler_params=pltpu.CompilerParams(
            collective_id=0, has_side_effects=True, vmem_limit_bytes=67043328 - 2 * right_side.size * 4
        ),
        name="solve",
    )(right_side, start_field, beam, noise, inv_power[None], smooth[None])
    return pl.pallas_call(
        write_out,
        out_shape=[jax.ShapeDtypeStruct(right_side.shape, F32)] * 2,
        in_specs=[vmem_spec] * 2,
        out_specs=[any_spec] * 2,
        scratch_shapes=[pltpu.SemaphoreType.DMA((2,))],
        compiler_params=pltpu.CompilerParams(vmem_limit_bytes=1024 * 1024),
        name="write_out",
    )(*outs)


def solution(mesh):
    in_specs = (
        P("ma", "freq", None, None),
        P("ma", "freq", None, None),
        P("ma", "freq", None, None, None),
        P("ma", "freq", None),
        P(),
        P(),
    )
    out_specs = (P("ma", "freq", None, None), P("ma", "freq", None, None))
    return jax.shard_map(shards, mesh=mesh, in_specs=in_specs, out_specs=out_specs, check_vma=False)
```

```python
import functools

import jax
import jax.numpy as jnp
from jax import lax
from jax.experimental import pallas as pl
from jax.experimental.pallas import tpu as pltpu
from jax.sharding import PartitionSpec as P

MESH = pl.DeviceIdType.MESH
F32, BF16 = jnp.float32, jnp.bfloat16


def split(x):
    high = x.astype(BF16)
    return high, (x - high.astype(F32)).astype(BF16)


def times(x, high, low, transposed):
    dims = (((1,), (1 if transposed else 0,)), ((), ()))
    rows = x.shape[0]
    x_high, x_low = split(x)
    both = jnp.concatenate([x_high, x_low], axis=0)
    main = lax.dot_general(both, high, dims, preferred_element_type=F32)
    rest = lax.dot_general(x_high, low, dims, preferred_element_type=F32)
    return main[:rows] + (main[rows:] + rest)


def kernel(
    nma, nf, rhs_in, x0_in, beam_in, noise_in, power_in, smooth_in, sol_s, res_s,
    rhs_s, x0_s, beam_s, noise_s, power_s, smooth_s,
    high_s, low_s, x_s, y_s, r_s, u_s, w_s, mask_s, halo_s, message_s, all_s,
    in_sem, beam_sem, halo_send, halo_recv, sum_send, sum_recv, word_sem,
):
    modes, freqs, _, ell = rhs_in.shape
    rank = beam_in.shape[3]
    width = modes * rank
    n = nma * nf
    my_ma, my_f = lax.axis_index("ma"), lax.axis_index("freq")
    me = my_ma * nf + my_f
    last = freqs - 1
    two_sided = nf > 2

    def at(g):
        return jnp.where(my_f == 0, last - g, g)


    x0_copy = pltpu.make_async_copy(x0_in, x0_s, in_sem.at[0])
    small = [
        pltpu.make_async_copy(power_in, power_s, in_sem.at[1]),
        pltpu.make_async_copy(smooth_in, smooth_s, in_sem.at[2]),
        pltpu.make_async_copy(noise_in, noise_s, in_sem.at[3]),
    ]
    rhs_copy = pltpu.make_async_copy(rhs_in, rhs_s, in_sem.at[4])
    x0_copy.start()
    for copy in small:
        copy.start()
    beam_copies = {}
    for f in range(freqs):
        beam_copies[f] = [
            pltpu.make_async_copy(beam_in.at[:, at(f), a], beam_s.at[f, a], beam_sem.at[2 * f + a])
            for a in range(2)
        ]
        for copy in beam_copies[f]:
            copy.start()
        if f == 0:
            rhs_copy.start()

    def target(offset):
        ma = my_ma + offset // nf
        other = my_f + offset % nf
        return lax.rem(ma, nma), lax.rem(other, nf)

    def partners(size, place):
        distances = [1 << bit for bit in range(size.bit_length() - 1)]
        return [place + d * (1 - 2 * (place // d % 2)) for d in distances]

    word = [(my_ma, other) for other in partners(nf, my_f)]
    word += [(other, my_f) for other in partners(nma, my_ma)]
    barrier = pltpu.get_barrier_semaphore()
    near = jnp.where(my_f == 0, 1, my_f - 1)
    has_far = (my_f > 0) & (my_f < nf - 1)

    def greet(device):
        pl.semaphore_signal(barrier, inc=1, device_id=device, device_id_type=MESH)

    for device in word:
        greet(device)
    expected = len(word)
    if nf > 2:
        pl.when(my_f > 0)(lambda: greet((my_ma, my_f - 1)))
        pl.when(my_f < nf - 1)(lambda: greet((my_ma, my_f + 1)))
        expected = expected + jnp.minimum(my_f, 1) + jnp.minimum(nf - 1 - my_f, 1)

    def pass_word(step):
        if step > 0:
            pl.semaphore_wait(word_sem.at[step - 1], 1)
        if step < len(word):
            pl.semaphore_signal(
                word_sem.at[step], inc=1, device_id=word[step], device_id_type=MESH
            )

    def near_copy(kind, source):
        side = jnp.minimum(my_f // 2, 1) if two_sided else 0
        return pltpu.make_async_remote_copy(
            src_ref=source.at[0], dst_ref=halo_s.at[kind, side],
            send_sem=halo_send.at[kind, 0], recv_sem=halo_recv.at[kind, side],
            device_id=(my_ma, near), device_id_type=MESH,
        )

    def far_copy(kind, source):
        return pltpu.make_async_remote_copy(
            src_ref=source.at[last], dst_ref=halo_s.at[kind, 0],
            send_sem=halo_send.at[kind, 1], recv_sem=halo_recv.at[kind, 0],
            device_id=(my_ma, my_f + 1), device_id_type=MESH,
        )

    def arrival(kind, side):
        slot = halo_s.at[kind, side]
        return pltpu.make_async_copy(slot, slot, halo_recv.at[kind, side])

    def send(kind, source):
        if nf > 1:
            near_copy(kind, source).start()
        if two_sided:
            pl.when(has_far)(lambda: far_copy(kind, source).start())

    def arrive(kind):
        if nf > 1:
            arrival(kind, 0).wait()
        if two_sided:
            pl.when(has_far)(lambda: arrival(kind, 1).wait())

    def sent(kind, source):
        if nf > 1:
            near_copy(kind, source).wait_send()
        if two_sided:
            pl.when(has_far)(lambda: far_copy(kind, source).wait_send())

    if nf == 1:
        halo_s[...] = jnp.zeros_like(halo_s)
    if two_sided:
        @pl.when(jnp.logical_not(has_far))
        def _():
            halo_s[:, 1] = jnp.zeros_like(halo_s[:, 1])

    x0_copy.wait()
    for f in range(freqs):
        for b in range(2):
            x_s[f, b * modes:(b + 1) * modes, :] = x0_s[:, at(f), b, :]
    for copy in small:
        copy.wait()
    pl.semaphore_wait(barrier, expected)
    send(0, x_s)
    pass_word(0)

    power, smooth = power_s[...], smooth_s[...]
    own = (
        lax.broadcasted_iota(jnp.int32, (modes, width), 1) // rank
        == lax.broadcasted_iota(jnp.int32, (modes, width), 0)
    )
    for f in range(freqs):
        mask_s[f] = jnp.where(own, jnp.concatenate([noise_s[:, at(f), :]] * modes, axis=1), 0.0)

    def project(f, field):
        seen = times(field, high_s[f], low_s[f], True)
        real = seen[:modes, :width] + seen[modes:, width:]
        imaginary = seen[modes:, :width] - seen[:modes, width:]
        return real, imaginary, mask_s[f] * real, mask_s[f] * imaginary

    def back(f, real, imaginary):
        weighted = jnp.concatenate(
            [
                jnp.concatenate([real, -imaginary], axis=1),
                jnp.concatenate([imaginary, real], axis=1),
            ],
            axis=0,
        )
        return times(weighted, high_s[f], low_s[f], False)

    def count(f):
        value = float(f > 0) + float(f < last) + float(nf > 1 and f == 0)
        if two_sided and f == last:
            value = value + jnp.where(has_far, 1.0, 0.0)
        return value

    def local_prior(f, ref):
        value = count(f) * ref[f]
        if f > 0:
            value = value - ref[f - 1]
        if f < last:
            value = value - ref[f + 1]
        return power * ref[f] + smooth * value

    def apply_beam(f, field):
        _, _, real, imaginary = project(f, field)
        return back(f, real, imaginary)

    steps = list(range(1, len(word) + 1))

    def advance():
        if steps:
            pass_word(steps.pop(0))

    edges = [0, last] if two_sided and last else [0]
    inner = [f for f in range(freqs) if f not in edges]
    for f in edges + inner:
        for copy in beam_copies[f]:
            copy.wait()
        high, low = split(beam_s[f].reshape(2 * width, ell))
        high_s[f] = high
        low_s[f] = low
        if f == 0:
            rhs_copy.wait()
        rhs = jnp.concatenate([rhs_s[:, at(f), 0, :], rhs_s[:, at(f), 1, :]], axis=0)
        y_s[f] = rhs - apply_beam(f, x_s[f]) - local_prior(f, x_s)
        if f == edges[-1]:
            send(1, y_s)
        elif f in inner:
            advance()
    for f in inner:
        r_s[f] = y_s[f]
        u_s[f] = apply_beam(f, r_s[f])
        advance()
    arrive(0)
    arrive(1)
    before = after = 0.0
    r_s[0] = y_s[0] + smooth * halo_s[0, 0]
    if nf > 1:
        before = halo_s[1, 0] + smooth * x_s[0]
    if two_sided:
        base = r_s if last == 0 else y_s
        r_s[last] = base[last] + smooth * halo_s[0, 1]
        after = jnp.where(has_far, halo_s[1, 1] + smooth * x_s[last], 0.0)
    for f in edges:
        value = apply_beam(f, r_s[f]) + local_prior(f, r_s)
        if f == 0:
            value = value - smooth * before
        if f == last:
            value = value - smooth * after
        u_s[f] = value
    send(2, u_s)
    for f in inner:
        u_s[f] = u_s[f] + local_prior(f, r_s)
    norm = jnp.zeros((2 * modes, ell), F32)
    curve, square, cube = norm, norm, norm
    beam_part = jnp.zeros((modes, width), F32)
    pending = {}
    for f in inner + edges:
        real, imaginary, real_weighted, imaginary_weighted = project(f, u_s[f])
        pending[f] = real_weighted, imaginary_weighted
        beam_part = beam_part + (real * real_weighted + imaginary * imaginary_weighted)
        w_s[f] = local_prior(f, u_s)
        norm = norm + r_s[f] * r_s[f]
        curve = curve + r_s[f] * u_s[f]
        square = square + u_s[f] * u_s[f]
        cube = cube + u_s[f] * w_s[f]
    arrive(2)
    before = smooth * halo_s[2, 0]
    cube = cube - before * u_s[0]
    if two_sided:
        after = smooth * halo_s[2, 1]
        cube = cube - after * u_s[last]
    lane = lax.broadcasted_iota(jnp.int32, (1, 128), 1)
    message = jnp.zeros((1, 128), F32)
    for i, part in enumerate((norm, curve, square, cube)):
        total = jnp.sum(part, keepdims=True)
        if i == 3:
            total = total + jnp.sum(beam_part, keepdims=True)
        message = jnp.where(lane == i, total, message)
    message_s[0] = message
    all_s[me] = message

    while steps:
        advance()

    def share(offset, carry):
        pltpu.make_async_remote_copy(
            src_ref=message_s.at[0], dst_ref=all_s.at[me], send_sem=sum_send, recv_sem=sum_recv,
            device_id=target(offset), device_id_type=MESH,
        ).start()
        return carry

    if n > 64:
        lax.fori_loop(1, n, share, 0)
    else:
        for offset in range(1, n):
            share(offset, 0)

    w_s[0] = w_s[0] - before
    if two_sided:
        w_s[last] = w_s[last] - after
    for f in range(freqs):
        w_s[f] = w_s[f] + back(f, *pending[f])
    for kind, source in enumerate((x_s, y_s, u_s)):
        sent(kind, source)
    if n > 1:
        everything = all_s.at[pl.ds(0, n - 1)]
        pltpu.make_async_copy(everything, everything, sum_recv).wait()
    total = jnp.sum(all_s[...], axis=0)
    m0, m1, m2, m3 = (total[:, i:i + 1] for i in range(4))
    step = m0 / m1
    norm_next = step * (step * m2 - m1)
    curve_next = m1 - 2.0 * step * m2 + step * step * m3
    growth = norm_next / m0
    step_next = norm_next / (curve_next - growth * norm_next / step)
    c = step + step_next * (1.0 + growth)
    e = step * step_next
    for f in range(freqs):
        solved = x_s[f] + c * r_s[f] - e * u_s[f]
        left = r_s[f] - c * u_s[f] + e * w_s[f]
        for b in range(2):
            sol_s[:, at(f), b, :] = solved[b * modes:(b + 1) * modes]
            res_s[:, at(f), b, :] = left[b * modes:(b + 1) * modes]
    if n > 1:
        everything = all_s.at[pl.ds(0, n - 1)]
        pltpu.make_async_copy(everything, everything, sum_send).wait()


def write_out(sol_in, res_in, sol_out, res_out, sem):
    copies = [
        pltpu.make_async_copy(sol_in, sol_out, sem.at[0]),
        pltpu.make_async_copy(res_in, res_out, sem.at[1]),
    ]
    for copy in copies:
        copy.start()
    for copy in copies:
        copy.wait()


def shards(right_side, start_field, beam, noise, inv_power, smooth):
    nma, nf = lax.axis_size("ma"), lax.axis_size("freq")
    modes, freqs, _, ell = right_side.shape
    rank = beam.shape[3]
    width = modes * rank
    vmem_spec = pl.BlockSpec(memory_space=pltpu.VMEM)
    any_spec = pl.BlockSpec(memory_space=pl.ANY)
    field = pltpu.VMEM(right_side.shape, F32)
    slab = pltpu.VMEM((freqs, 2 * modes, ell), F32)
    half = pltpu.VMEM((freqs, 2 * width, ell), BF16)
    outs = pl.pallas_call(
        functools.partial(kernel, nma, nf),
        out_shape=[field] * 2,
        in_specs=[any_spec] * 6,
        out_specs=[vmem_spec] * 2,
        scratch_shapes=[
            field, field,
            pltpu.VMEM((freqs, 2, modes, rank, ell), F32),
            pltpu.VMEM(noise.shape, F32),
            pltpu.VMEM((1, ell), F32), pltpu.VMEM((1, ell), F32),
            half, half,
            slab, slab, slab, slab, slab,
            pltpu.VMEM((freqs, modes, width), F32),
            pltpu.VMEM((3, 2, 2 * modes, ell), F32),
            pltpu.VMEM((1, 1, 128), F32),
            pltpu.VMEM((nma * nf, 1, 128), F32),
            pltpu.SemaphoreType.DMA((5,)),
            pltpu.SemaphoreType.DMA((2 * freqs,)),
            pltpu.SemaphoreType.DMA((3, 2)),
            pltpu.SemaphoreType.DMA((3, 2)),
            pltpu.SemaphoreType.DMA,
            pltpu.SemaphoreType.DMA,
            pltpu.SemaphoreType.REGULAR(((nma * nf).bit_length(),)),
        ],
        compiler_params=pltpu.CompilerParams(
            collective_id=0, has_side_effects=True, vmem_limit_bytes=67043328 - 2 * right_side.size * 4
        ),
        name="solve",
    )(right_side, start_field, beam, noise, inv_power[None], smooth[None])
    return pl.pallas_call(
        write_out,
        out_shape=[jax.ShapeDtypeStruct(right_side.shape, F32)] * 2,
        in_specs=[vmem_spec] * 2,
        out_specs=[any_spec] * 2,
        scratch_shapes=[pltpu.SemaphoreType.DMA((2,))],
        compiler_params=pltpu.CompilerParams(vmem_limit_bytes=1024 * 1024),
        name="write_out",
    )(*outs)


def solution(mesh):
    in_specs = (
        P("ma", "freq", None, None),
        P("ma", "freq", None, None),
        P("ma", "freq", None, None, None),
        P("ma", "freq", None),
        P(),
        P(),
    )
    out_specs = (P("ma", "freq", None, None), P("ma", "freq", None, None))
    return jax.shard_map(shards, mesh=mesh, in_specs=in_specs, out_specs=out_specs, check_vma=False)
```
